32 devices in a mesh: gx: 4 (over y, x), gy: 8 (over z, core).
Axes of the slice: x: 2, y: 2, z: 4, core: 2. Of those that a mesh axis runs over, the one named last changes fastest.
Arguments:
- dist_start: float32 [19, 2, 512, 1024], P(None, None, 'gx', 'gy'), may hold values from -6 to 6
- cotangent: float32 [19, 2, 512, 1024], P(None, None, 'gx', 'gy'), may hold values from -6 to 6
- solid_mask: int32 [2, 512, 1024], P(None, 'gx', 'gy'), may hold values 0 or 1
- weight_in: bfloat16 [19, 128], replicated, may hold values from -1.25 to 1.25
- bias_in: float32 [128], replicated, may hold values from -3 to 3
- weight_out: bfloat16 [128, 19], replicated, may hold values from -0.5 to 0.5
- bias_out: float32 [19], replicated, may hold values from -3 to 3
Outputs:
- grad_start: float32 [19, 2, 512, 1024], P(None, None, 'gx', 'gy')
- grad_weight_in: float32 [19, 128], replicated
- grad_bias_in: float32 [128], replicated
- grad_weight_out: float32 [128, 19], replicated
- grad_bias_out: float32 [19], replicated
The draws below stay inside these ranges and needn't reach their ends.
Inputs may be any that keep to these rules, and one draw needn't show every extreme that they name: `solid_mask`: 1 marks a solid cell.
All inputs are finite; a program needn't handle non-finite values. No bound on the sum of `solid_mask` on one device may be relied on, other than what follows from the above.
Results may differ from the reference program's by a relative error of at most 0.0067.
Values may be sent and summed in bfloat16 or wider, within the bound.
A program may use at most 256 MiB of HBM per device.

```python
import math
import jax
import jax.numpy as jnp
import numpy as np
from jax import lax

Q = 19
H = 128
NZ = 2
NX = 512
NY = 1024
CELLS = 1048576


def plant(values, rng, low, top_value):
    place = [jax.random.randint(jax.random.fold_in(rng, axis), (), 0, length) for axis, length in enumerate(values.shape)]
    widest = values.shape.index(max(values.shape))
    next_to = place[:widest] + [(place[widest] + 1) % values.shape[widest]] + place[widest + 1:]
    return values.at[tuple(place)].set(low).at[tuple(next_to)].set(top_value)


def steps_of(stream_key, shape, split, least, high):
    factor_of = 1.0
    for dim, blocks in split:
        draws = jax.random.uniform(jax.random.fold_in(jax.random.fold_in(stream_key, 6), dim), (blocks,), jnp.float32, least / len(split), high / len(split))
        factor_of = factor_of * jnp.repeat(jnp.exp(draws), shape[dim] // blocks).reshape((-1,) + (1,) * (len(shape) - 1 - dim))
    return factor_of


def bell_draw(own_key, dims, spread, bound, cuts=(), kind=jnp.bfloat16):
    values = spread * jax.random.normal(own_key, dims, jnp.float32)
    if cuts:
        values = values * steps_of(own_key, dims, cuts, -0.22, 0.18)
    return jnp.clip(values, -bound, bound).astype(kind)


def setup_inputs(seed: int = 0) -> dict:
    arg_keys = jax.random.split(jax.random.key(seed), 8)
    dist_start = bell_draw(arg_keys[0], (Q, NZ, NX, NY), 1.0, 6.0, ((2, 4), (3, 8)), jnp.float32)
    cotangent = bell_draw(arg_keys[1], (Q, NZ, NX, NY), 1.0, 6.0, ((2, 4), (3, 8)), jnp.float32)
    solid_mask = plant((jax.random.randint(arg_keys[2], (NZ, NX, NY), 0, 4) < 1).astype(jnp.int32), jax.random.fold_in(arg_keys[2], 1), 0, 1)
    weight_in = bell_draw(arg_keys[3], (Q, H), Q ** -0.5, 1.25)
    bias_in = bell_draw(arg_keys[4], (H,), 0.5, 3.0, (), jnp.float32)
    weight_out = bell_draw(arg_keys[5], (H, Q), H ** -0.5, 0.5)
    bias_out = bell_draw(arg_keys[6], (Q,), 0.5, 3.0, (), jnp.float32)
    return {"dist_start": dist_start, "cotangent": cotangent, "solid_mask": solid_mask, "weight_in": weight_in, "bias_in": bias_in, "weight_out": weight_out, "bias_out": bias_out}


velocities = ((0, 0, 0), (1, 0, 0), (-1, 0, 0), (0, 1, 0), (0, -1, 0), (0, 0, 1), (0, 0, -1), (1, 1, 0), (-1, -1, 0), (1, -1, 0), (-1, 1, 0), (1, 0, 1), (-1, 0, -1), (1, 0, -1), (-1, 0, 1), (0, 1, 1), (0, -1, -1), (0, 1, -1), (0, -1, 1))
opposite = (0, 2, 1, 4, 3, 6, 5, 8, 7, 10, 9, 12, 11, 14, 13, 16, 15, 18, 17)

def stream(density, orient):
    pieces = []
    for component in range(19):
        move_x, move_y, move_z = velocities[component]
        pieces.append(jnp.roll(density[component], (orient * move_z, orient * move_x, orient * move_y), axis=(0, 1, 2)))
    return jnp.stack(pieces)

def hidden_of(flat_bf, weight_in, bias_in):
    preact = jnp.einsum('qh,qc->hc', weight_in.astype(jnp.float32), flat_bf.astype(jnp.float32)) + bias_in[:, None]
    return jnp.tanh(preact)

def collide_block(flat_cells, solid_flat, weight_in, bias_in, weight_out, bias_out):
    flat_bf = lax.optimization_barrier(flat_cells.astype(jnp.bfloat16))
    active = lax.optimization_barrier(hidden_of(flat_bf, weight_in, bias_in).astype(jnp.bfloat16))
    output = jnp.einsum('hq,hc->qc', weight_out.astype(jnp.float32), active.astype(jnp.float32)) + bias_out[:, None]
    bounced = flat_cells[np.array(opposite)]
    return jnp.where(solid_flat[None, :] > 0, bounced, flat_cells + output)

def backward_block(flat_cells, solid_flat, grad_post, weight_in, bias_in, weight_out):
    flat_bf = lax.optimization_barrier(flat_cells.astype(jnp.bfloat16))
    tanh_val = hidden_of(flat_bf, weight_in, bias_in)
    active = lax.optimization_barrier(tanh_val.astype(jnp.bfloat16))
    is_solid = solid_flat[None, :] > 0
    out_grad = jnp.where(is_solid, jnp.float32(0.0), grad_post)
    out_bf = lax.optimization_barrier(out_grad.astype(jnp.bfloat16))
    hid_grad = jnp.einsum('hq,qc->hc', weight_out.astype(jnp.float32), out_bf.astype(jnp.float32)) * (1.0 - tanh_val * tanh_val)
    hid_bf = lax.optimization_barrier(hid_grad.astype(jnp.bfloat16))
    in_grad = out_grad + jnp.einsum('qh,hc->qc', weight_in.astype(jnp.float32), hid_bf.astype(jnp.float32))
    in_grad = in_grad + jnp.where(is_solid, grad_post[np.array(opposite)], jnp.float32(0.0))
    d_weight_in = jnp.einsum('qc,hc->qh', flat_bf.astype(jnp.float32), hid_bf.astype(jnp.float32))
    d_bias_in = lax.optimization_barrier(jnp.sum(hid_grad, axis=1))
    d_weight_out = jnp.einsum('hc,qc->hq', active.astype(jnp.float32), out_bf.astype(jnp.float32))
    d_bias_out = lax.optimization_barrier(jnp.sum(out_grad, axis=1))
    return (in_grad, (d_weight_in, d_bias_in, d_weight_out, d_bias_out))

def to_blocks(flat_cells, block):
    return jnp.transpose(flat_cells.reshape(flat_cells.shape[0], -1, block), (1, 0, 2))

def from_blocks(blocks):
    return jnp.transpose(blocks, (1, 0, 2)).reshape(blocks.shape[1], -1)

def collide(density, solid_mask, weight_in, bias_in, weight_out, bias_out):
    total = solid_mask.size
    block = math.gcd(total, 65536)
    flat_blocks = to_blocks(density.reshape(density.shape[0], -1), block)
    solid_blocks = solid_mask.reshape(-1, block)

    def one_block(pair):
        return collide_block(pair[0], pair[1], weight_in, bias_in, weight_out, bias_out)
    posts = lax.map(one_block, (flat_blocks, solid_blocks))
    return from_blocks(posts).reshape(density.shape)

def backward(density, solid_mask, grad_post, weight_in, bias_in, weight_out):
    total = solid_mask.size
    block = math.gcd(total, 65536)
    flat_blocks = to_blocks(density.reshape(density.shape[0], -1), block)
    grad_blocks = to_blocks(grad_post.reshape(grad_post.shape[0], -1), block)
    solid_blocks = solid_mask.reshape(-1, block)
    number = density.shape[0]
    hidden = weight_in.shape[1]
    start = (jnp.zeros((number, hidden), jnp.float32), jnp.zeros((hidden,), jnp.float32), jnp.zeros((hidden, number), jnp.float32), jnp.zeros((number,), jnp.float32))

    def one_block(carry, triple):
        in_grad, parts = backward_block(triple[0], triple[1], triple[2], weight_in, bias_in, weight_out)
        return (tuple((carry[i] + parts[i] for i in range(4))), in_grad)
    totals, in_grads = lax.scan(one_block, start, (flat_blocks, solid_blocks, grad_blocks))
    return (from_blocks(in_grads).reshape(density.shape), totals)

def reference(dist_start, cotangent, solid_mask, weight_in, bias_in, weight_out, bias_out):
    post_start = collide(dist_start, solid_mask, weight_in, bias_in, weight_out, bias_out).astype(jnp.bfloat16)
    dist_middle = stream(post_start, 1)
    grad_post_middle = stream(cotangent, -1)
    grad_middle, partials_late = backward(dist_middle, solid_mask, grad_post_middle, weight_in, bias_in, weight_out)
    grad_post_start = stream(grad_middle, -1)
    grad_start, partials_early = backward(dist_start, solid_mask, grad_post_start, weight_in, bias_in, weight_out)
    factor = 1.0 / math.sqrt(CELLS)
    return (grad_start, (partials_early[0] + partials_late[0]) * factor, (partials_early[1] + partials_late[1]) * factor, (partials_early[2] + partials_late[2]) * factor, (partials_early[3] + partials_late[3]) * factor)
```

```python
import functools
import math

import jax
import jax.numpy as jnp
import numpy as np
from jax import lax
from jax.experimental import pallas as pl
from jax.experimental.pallas import tpu as pltpu
from jax.sharding import PartitionSpec as P

velocities = (
    (0, 0, 0),
    (1, 0, 0),
    (-1, 0, 0),
    (0, 1, 0),
    (0, -1, 0),
    (0, 0, 1),
    (0, 0, -1),
    (1, 1, 0),
    (-1, -1, 0),
    (1, -1, 0),
    (-1, 1, 0),
    (1, 0, 1),
    (-1, 0, -1),
    (1, 0, -1),
    (-1, 0, 1),
    (0, 1, 1),
    (0, -1, -1),
    (0, 1, -1),
    (0, -1, 1),
)
opposite = (0, 2, 1, 4, 3, 6, 5, 8, 7, 10, 9, 12, 11, 14, 13, 16, 15, 18, 17)
Q = 19
T = 8
KQ = Q * T
KA = KQ + 24
PAD = 8

PLUS_X = tuple(q for q in range(Q) if velocities[q][0] == 1)
MINUS_X = tuple(q for q in range(Q) if velocities[q][0] == -1)
REST = tuple(q for q in range(Q) if velocities[q][0] == 0)
SLOT = {q: s for s, q in enumerate(PLUS_X + MINUS_X + REST)}
NX5 = len(PLUS_X)
SIDE_Y = {
    1: tuple(q for q in range(Q) if velocities[q][1] == 1),
    -1: tuple(q for q in range(Q) if velocities[q][1] == -1),
}
MESH = pl.DeviceIdType.MESH


def kernel(
    nx,
    ny,
    factor,
    dist,
    cot,
    solid,
    first_in,
    first_out,
    second_out,
    second_in,
    bias_out,
    grad_start,
    sums,
    post_f,
    cot_f,
    mid_f,
    edge,
    halo,
    saved,
    a_in,
    a_out,
    b_out,
    b_in,
    act_s,
    hid_s,
    acc_in,
    acc_out,
    acc_bias,
    part_x,
    part_y,
    all_x,
    all_y,
    send_sem,
    recv_sem,
    sx_sem,
    rx_sem,
    sy_sem,
    ry_sem,
):
    me_x, me_y = lax.axis_index("gx"), lax.axis_index("gy")
    rows = dist.shape[2]
    tiles = rows // T
    H = first_in.shape[0]
    lanes = dist.shape[3]
    right_x, left_x = lax.rem(me_x + 1, nx), lax.rem(me_x + nx - 1, nx)
    right_y, left_y = lax.rem(me_y + 1, ny), lax.rem(me_y + ny - 1, ny)

    barrier = pltpu.get_barrier_semaphore()
    others = [(lax.rem(me_x + d, nx), me_y) for d in range(1, nx)]
    others += [(me_x, lax.rem(me_y + d, ny)) for d in range(1, ny)]
    others += [(a, b) for a in (left_x, right_x) for b in (left_y, right_y)]
    for other in others:
        pl.semaphore_signal(barrier, inc=1, device_id=other, device_id_type=MESH)

    col = lax.broadcasted_iota(jnp.int32, (H, KA), 1)
    row = lax.broadcasted_iota(jnp.int32, (KQ, H), 0)
    for s in range(T):
        keep = (col >= KQ) | ((col & (T - 1)) == s)
        a_in[s * H : (s + 1) * H, :] = jnp.where(keep, first_in[...], 0.0).astype(jnp.bfloat16)
        a_out[s * H : (s + 1) * H, :] = jnp.where(keep, first_out[...], 0.0).astype(jnp.bfloat16)
        mine = (row & (T - 1)) == s
        b_out[:, s * H : (s + 1) * H] = jnp.where(mine, second_out[...], 0.0).astype(jnp.bfloat16)
        b_in[:, s * H : (s + 1) * H] = jnp.where(mine, second_in[...], 0.0).astype(jnp.bfloat16)
    acc_in[...] = jnp.zeros_like(acc_in)
    acc_out[...] = jnp.zeros_like(acc_out)
    acc_bias[...] = jnp.zeros_like(acc_bias)

    lane = lax.broadcasted_iota(jnp.int32, (T, lanes), 1)

    def both(read):
        return jnp.concatenate([read(0), read(1)], axis=1)

    def widen(pieces, ones):
        tail = [jnp.full((T, 2 * lanes), ones, jnp.float32), jnp.zeros((2 * T, 2 * lanes), jnp.float32)]
        return jnp.concatenate(list(pieces) + tail, axis=0).astype(jnp.bfloat16)

    def put(field, number, orient, i, values):
        begin = pl.multiple_of(i * T, T)
        for q in range(Q):
            for z in range(2):
                field[SLOT[q], z, pl.ds(begin + PAD, T), :] = values[q][:, z * lanes : (z + 1) * lanes]
        for side in range(2):
            step = 1 - 2 * side
            columns = jnp.zeros((T, lanes), jnp.float32)
            for k, q in enumerate(SIDE_Y[orient * step]):
                for z in range(2):
                    at = z * lanes + (lanes - 1 if step == 1 else 0)
                    columns = jnp.where(lane == 2 * k + z, values[q][:, at : at + 1], columns)
            edge[number, side, pl.ds(begin, T), :] = columns

    def copies(field, number, orient):
        high, low = (0, NX5) if orient == 1 else (NX5, 0)
        last = rows + PAD
        pairs = [
            (field.at[pl.ds(high, NX5), :, pl.ds(rows, PAD), :], field.at[pl.ds(high, NX5), :, pl.ds(0, PAD), :], (right_x, me_y)),
            (field.at[pl.ds(low, NX5), :, pl.ds(PAD, PAD), :], field.at[pl.ds(low, NX5), :, pl.ds(last, PAD), :], (left_x, me_y)),
        ]
        for side, target in ((0, right_y), (1, left_y)):
            source, sink = edge.at[number, side], halo.at[number, side]
            pairs += [
                (source, sink.at[pl.ds(PAD, rows), :], (me_x, target)),
                (source.at[pl.ds(rows - PAD, PAD), :], sink.at[pl.ds(0, PAD), :], (right_x, target)),
                (source.at[pl.ds(0, PAD), :], sink.at[pl.ds(last, PAD), :], (left_x, target)),
            ]
        return [
            pltpu.make_async_remote_copy(
                src_ref=source,
                dst_ref=sink,
                send_sem=send_sem.at[number, n],
                recv_sem=recv_sem.at[number, n],
                device_id=target,
                device_id_type=MESH,
            )
            for n, (source, sink, target) in enumerate(pairs)
        ]

    def running(field, number, orient, i):
        pieces = []
        for q in range(Q):
            move_x, move_y, move_z = velocities[q]
            begin = i * T + PAD - orient * move_x
            if move_x == 0:
                begin = pl.multiple_of(begin, T)
            step = orient * move_y
            halves = []
            for z in range(2):
                from_z = (z + move_z) % 2
                tile = field[SLOT[q], from_z, pl.ds(begin, T), :]
                if step:
                    side = 0 if step == 1 else 1
                    k = 2 * SIDE_Y[move_y].index(q) + from_z
                    columns = halo[number, side, pl.ds(begin, T), :]
                    tile = pltpu.roll(tile, 1 if step == 1 else lanes - 1, 1)
                    tile = jnp.where(lane == (0 if step == 1 else lanes - 1), columns[:, k : k + 1], tile)
                halves.append(tile)
            pieces.append(jnp.concatenate(halves, axis=1))
        return pieces

    def own(i):
        begin = pl.multiple_of(i * T, T)
        return [both(lambda z: dist[q, z, pl.ds(begin, T), :]) for q in range(Q)]

    def solid_of(i):
        begin = pl.multiple_of(i * T, T)
        return both(lambda z: solid[z, pl.ds(begin, T), :]) > 0

    CH = 2 * H

    def dot(a, b):
        return jnp.dot(a, b, preferred_element_type=jnp.float32)

    def dot_t(a, b):
        return lax.dot_general(a, b, (((1,), (1,)), ((), ())), preferred_element_type=jnp.float32)

    def take(i, carry):
        begin = pl.multiple_of(i * T, T)
        put(cot_f, 0, -1, i, [both(lambda z: cot[q, z, pl.ds(begin, T), :]) for q in range(Q)])
        return carry

    lax.fori_loop(0, tiles, take, 0)
    pl.semaphore_wait(barrier, len(others))
    first = copies(cot_f, 0, -1)
    for copy in first:
        copy.start()

    def collide(i, carry):
        field = own(i)
        wide = widen(field, 1.0)
        for c in range(T * H // CH):
            part = slice(c * CH, (c + 1) * CH)
            saved[i, part, :] = jnp.tanh(dot(a_in[part, :], wide)).astype(jnp.bfloat16)
        out = dot(b_out[...], saved[i])
        is_solid = solid_of(i)
        posts = []
        for q in range(Q):
            at = slice(q * T, (q + 1) * T)
            value = field[q] + (out[at] + bias_out[at, :])
            value = jnp.where(is_solid, field[opposite[q]], value)
            posts.append(value.astype(jnp.bfloat16).astype(jnp.float32))
        put(post_f, 1, 1, i, posts)
        return carry

    lax.fori_loop(0, tiles, collide, 0)
    second = copies(post_f, 1, 1)
    for copy in second:
        copy.start()
    for copy in first + second:
        copy.wait()

    def backward(i, wide, grad, act_of):
        is_solid = solid_of(i)
        masked = [jnp.where(is_solid, 0.0, g) for g in grad]
        wide_out = widen(masked, 0.0)
        for c in range(T * H // CH):
            part = slice(c * CH, (c + 1) * CH)
            t = act_of(part)
            hid = dot(a_out[part, :], wide_out) * (1.0 - t * t)
            hid = hid.astype(jnp.bfloat16)
            hid_s[part, :] = hid
            acc_in[:, part] += dot_t(wide, hid)
        into = dot(b_in[...], hid_s[...])
        results = []
        for q in range(Q):
            at = slice(q * T, (q + 1) * T)
            acc_bias[at, :] += masked[q]
            results.append(masked[q] + into[at] + jnp.where(is_solid, grad[opposite[q]], 0.0))
        return wide_out, results

    def late(i, carry):
        wide = widen(running(post_f, 1, 1, i), 1.0)

        def act_of(part):
            t = jnp.tanh(dot(a_in[part, :], wide))
            act_s[part, :] = t.astype(jnp.bfloat16)
            return t

        wide_out, results = backward(i, wide, running(cot_f, 0, -1, i), act_of)
        for c in range(T * H // CH):
            part = slice(c * CH, (c + 1) * CH)
            acc_out[:, part] += dot_t(wide_out, act_s[part, :])
        put(mid_f, 2, -1, i, results)
        return carry

    lax.fori_loop(0, tiles, late, 0)
    third = copies(mid_f, 2, -1)
    for copy in third:
        copy.start()
    for copy in third:
        copy.wait()

    def early(i, carry):
        wide = widen(own(i), 1.0)
        wide_out, results = backward(
            i, wide, running(mid_f, 2, -1, i), lambda part: saved[i, part, :].astype(jnp.float32)
        )
        for c in range(T * H // CH):
            part = slice(c * CH, (c + 1) * CH)
            acc_out[:, part] += dot_t(wide_out, saved[i, part, :])
        begin = pl.multiple_of(i * T, T)
        for q in range(Q):
            for z in range(2):
                grad_start[q, z, pl.ds(begin, T), :] = results[q][:, z * lanes : (z + 1) * lanes]
        return carry

    lax.fori_loop(0, tiles, early, 0)

    tall = lax.broadcasted_iota(jnp.int32, (KA, H), 0) & (T - 1)

    def diagonal(acc):
        total = jnp.zeros((KA, H), jnp.float32)
        for s in range(T):
            total += jnp.where(tall == s, acc[:, s * H : (s + 1) * H], 0.0)
        return jnp.sum(total.reshape(KA // T, T, H), axis=1)

    part_x[...] = jnp.zeros_like(part_x)
    part_x[0 : KA // T, :] = diagonal(acc_in)
    part_x[24 : 24 + KA // T, :] = diagonal(acc_out)
    bias = jnp.sum(acc_bias[...], axis=1, keepdims=True)
    bias = jnp.broadcast_to(bias, (KQ, H)).reshape(Q, T, H)
    part_x[48 : 48 + Q, :] = jnp.sum(bias, axis=1)

    def gather(part, everyone, size, me, place, s_sem, r_sem):
        sends = [
            pltpu.make_async_remote_copy(
                src_ref=part,
                dst_ref=everyone.at[me],
                send_sem=s_sem.at[d - 1],
                recv_sem=r_sem.at[d - 1],
                device_id=place(lax.rem(me + d, size)),
                device_id_type=MESH,
            )
            for d in range(1, size)
        ]
        for copy in sends:
            copy.start()
        everyone[me] = part[...]
        for copy in sends:
            copy.wait()
        total = everyone[0]
        for d in range(1, size):
            total = total + everyone[d]
        return total

    part_y[...] = gather(part_x, all_x, nx, me_x, lambda a: (a, me_y), sx_sem, rx_sem)
    sums[...] = gather(part_y, all_y, ny, me_y, lambda b: (me_x, b), sy_sem, ry_sem) * factor


def shards(dist_start, cotangent, solid_mask, weight_in, bias_in, weight_out, bias_out):
    nx, ny = lax.axis_size("gx"), lax.axis_size("gy")
    H = weight_in.shape[1]
    rows, lanes = dist_start.shape[2:]
    tiles = rows // T
    f32, bf16 = jnp.float32, jnp.bfloat16
    factor = 1.0 / math.sqrt(solid_mask.size * nx * ny)

    def top(x):
        return lax.reduce_precision(x, 8, 7)

    one = top(bias_in)
    two = top(bias_in - one)
    three = top(bias_in - one - two)
    biases = jnp.stack([one, two, three], axis=1)
    w_in, w_out = weight_in.astype(f32), weight_out.astype(f32)
    first_in = jnp.concatenate(
        [jnp.repeat(w_in.T, T, axis=1), biases, jnp.zeros((H, KA - KQ - 3), f32)], axis=1
    )
    first_out = jnp.concatenate([jnp.repeat(w_out, T, axis=1), jnp.zeros((H, KA - KQ), f32)], axis=1)
    second_out = jnp.repeat(w_out.T, T, axis=0)
    second_in = jnp.repeat(w_in, T, axis=0)
    bias_col = jnp.repeat(bias_out, T)[:, None]

    field = pltpu.VMEM((Q, 2, rows + 2 * PAD, lanes), f32)
    vmem = pl.BlockSpec(memory_space=pltpu.VMEM)
    dma = pltpu.SemaphoreType.DMA
    grad_start, sums = pl.pallas_call(
        functools.partial(kernel, nx, ny, factor),
        out_shape=(
            jax.ShapeDtypeStruct(dist_start.shape, f32),
            jax.ShapeDtypeStruct((72, H), f32),
        ),
        in_specs=[vmem] * 8,
        out_specs=(vmem, vmem),
        scratch_shapes=[
            field,
            field,
            field,
            pltpu.VMEM((3, 2, rows, lanes), f32),
            pltpu.VMEM((3, 2, rows + 2 * PAD, lanes), f32),
            pltpu.VMEM((tiles, T * H, 2 * lanes), bf16),
            pltpu.VMEM((T * H, KA), bf16),
            pltpu.VMEM((T * H, KA), bf16),
            pltpu.VMEM((KQ, T * H), bf16),
            pltpu.VMEM((KQ, T * H), bf16),
            pltpu.VMEM((T * H, 2 * lanes), bf16),
            pltpu.VMEM((T * H, 2 * lanes), bf16),
            pltpu.VMEM((KA, T * H), f32),
            pltpu.VMEM((KA, T * H), f32),
            pltpu.VMEM((KQ, 2 * lanes), f32),
            pltpu.VMEM((72, H), f32),
            pltpu.VMEM((72, H), f32),
            pltpu.VMEM((nx, 72, H), f32),
            pltpu.VMEM((ny, 72, H), f32),
            dma((3, 8)),
            dma((3, 8)),
            dma((nx - 1,)),
            dma((nx - 1,)),
            dma((ny - 1,)),
            dma((ny - 1,)),
        ],
        compiler_params=pltpu.CompilerParams(
            collective_id=0, has_side_effects=True, vmem_limit_bytes=60 * 1024 * 1024
        ),
    )(dist_start, cotangent, solid_mask, first_in, first_out, second_out, second_in, bias_col)
    return (
        grad_start,
        sums[0:Q],
        sums[Q],
        sums[24 : 24 + Q].T,
        sums[48 : 48 + Q, 0],
    )


def solution(mesh):
    placed = (
        P(None, None, "gx", "gy"),
        P(None, None, "gx", "gy"),
        P(None, "gx", "gy"),
        P(),
        P(),
        P(),
        P(),
    )
    return jax.shard_map(
        shards,
        mesh=mesh,
        in_specs=placed,
        out_specs=(P(None, None, "gx", "gy"), P(), P(), P(), P()),
        check_vma=False,
    )
```

```python
import functools
import math

import jax
import jax.numpy as jnp
import numpy as np
from jax import lax
from jax.experimental import pallas as pl
from jax.experimental.pallas import tpu as pltpu
from jax.sharding import PartitionSpec as P

velocities = (
    (0, 0, 0),
    (1, 0, 0),
    (-1, 0, 0),
    (0, 1, 0),
    (0, -1, 0),
    (0, 0, 1),
    (0, 0, -1),
    (1, 1, 0),
    (-1, -1, 0),
    (1, -1, 0),
    (-1, 1, 0),
    (1, 0, 1),
    (-1, 0, -1),
    (1, 0, -1),
    (-1, 0, 1),
    (0, 1, 1),
    (0, -1, -1),
    (0, 1, -1),
    (0, -1, 1),
)
opposite = (0, 2, 1, 4, 3, 6, 5, 8, 7, 10, 9, 12, 11, 14, 13, 16, 15, 18, 17)
Q = 19
T = 8
KQ = Q * T
KA = KQ + 24
PAD = 8

PLUS_X = tuple(q for q in range(Q) if velocities[q][0] == 1)
MINUS_X = tuple(q for q in range(Q) if velocities[q][0] == -1)
REST = tuple(q for q in range(Q) if velocities[q][0] == 0)
SLOT = {q: s for s, q in enumerate(PLUS_X + MINUS_X + REST)}
NX5 = len(PLUS_X)
SIDE_Y = {
    1: tuple(q for q in range(Q) if velocities[q][1] == 1),
    -1: tuple(q for q in range(Q) if velocities[q][1] == -1),
}
MESH = pl.DeviceIdType.MESH


def kernel(
    nx,
    ny,
    factor,
    dist,
    cot,
    solid,
    weight_in,
    bias_in,
    weight_out,
    bias_row,
    grad_start,
    grad_weight_in,
    grad_bias_in,
    grad_weight_out,
    grad_bias_out,
    post_f,
    cot_f,
    mid_f,
    edge,
    halo,
    saved,
    a_in,
    a_out,
    b_out,
    b_in,
    act_s,
    hid_s,
    acc_in,
    acc_out,
    acc_bias,
    bias_out,
    part_x,
    part_y,
    all_x,
    all_y,
    send_sem,
    recv_sem,
    sx_sem,
    rx_sem,
    sy_sem,
    ry_sem,
):
    me_x, me_y = lax.axis_index("gx"), lax.axis_index("gy")
    rows = dist.shape[2]
    tiles = rows // T
    H = weight_in.shape[1]
    lanes = dist.shape[3]
    right_x, left_x = lax.rem(me_x + 1, nx), lax.rem(me_x + nx - 1, nx)
    right_y, left_y = lax.rem(me_y + 1, ny), lax.rem(me_y + ny - 1, ny)

    barrier = pltpu.get_barrier_semaphore()
    others = [(lax.rem(me_x + d, nx), me_y) for d in range(1, nx)]
    others += [(me_x, lax.rem(me_y + d, ny)) for d in range(1, ny)]
    others += [(a, b) for a in (left_x, right_x) for b in (left_y, right_y)]
    for other in others:
        pl.semaphore_signal(barrier, inc=1, device_id=other, device_id_type=MESH)

    ident = lax.broadcasted_iota(jnp.int32, (2 * H, Q), 0) >> 3
    repeat = jnp.where(ident == lax.broadcasted_iota(jnp.int32, (2 * H, Q), 1), 1.0, 0.0)
    spread = repeat.astype(jnp.bfloat16)
    tall_in = jnp.dot(spread, weight_in[...], preferred_element_type=jnp.float32)
    tall_out = lax.dot_general(
        spread, weight_out[...], (((1,), (1,)), ((), ())), preferred_element_type=jnp.float32
    )
    second_in, second_out = tall_in[:KQ], tall_out[:KQ]
    left = bias_in[...]
    place = lax.broadcasted_iota(jnp.int32, (2 * H, H), 0)
    for n in range(3):
        addend = left.astype(jnp.bfloat16).astype(jnp.float32)
        tall_in = jnp.where(place == KQ + n, addend, tall_in)
        left = left - addend
    first_in = jnp.transpose(tall_in)[:, :KA]
    first_out = jnp.transpose(tall_out)[:, :KA]
    column = jnp.sum(repeat[:KQ] * bias_row[...], axis=1, keepdims=True)
    bias_out[...] = jnp.broadcast_to(column, bias_out.shape)
    col = lax.broadcasted_iota(jnp.int32, (H, KA), 1)
    row = lax.broadcasted_iota(jnp.int32, (KQ, H), 0)
    for s in range(T):
        keep = (col >= KQ) | ((col & (T - 1)) == s)
        a_in[s * H : (s + 1) * H, :] = jnp.where(keep, first_in, 0.0).astype(jnp.bfloat16)
        a_out[s * H : (s + 1) * H, :] = jnp.where(keep, first_out, 0.0).astype(jnp.bfloat16)
        mine = (row & (T - 1)) == s
        b_out[:, s * H : (s + 1) * H] = jnp.where(mine, second_out, 0.0).astype(jnp.bfloat16)
        b_in[:, s * H : (s + 1) * H] = jnp.where(mine, second_in, 0.0).astype(jnp.bfloat16)
    acc_in[...] = jnp.zeros_like(acc_in)
    acc_out[...] = jnp.zeros_like(acc_out)
    acc_bias[...] = jnp.zeros_like(acc_bias)

    lane = lax.broadcasted_iota(jnp.int32, (T, lanes), 1)

    def both(read):
        return jnp.concatenate([read(0), read(1)], axis=1)

    def widen(pieces, ones):
        tail = [jnp.full((T, 2 * lanes), ones, jnp.float32), jnp.zeros((2 * T, 2 * lanes), jnp.float32)]
        return jnp.concatenate(list(pieces) + tail, axis=0).astype(jnp.bfloat16)

    def put(field, number, orient, i, values):
        begin = pl.multiple_of(i * T, T)
        for q in range(Q):
            for z in range(2):
                field[SLOT[q], z, pl.ds(begin + PAD, T), :] = values[q][:, z * lanes : (z + 1) * lanes]
        for side in range(2):
            step = 1 - 2 * side
            columns = jnp.zeros((T, lanes), jnp.float32)
            for k, q in enumerate(SIDE_Y[orient * step]):
                for z in range(2):
                    at = z * lanes + (lanes - 1 if step == 1 else 0)
                    columns = jnp.where(lane == 2 * k + z, values[q][:, at : at + 1], columns)
            edge[number, side, pl.ds(begin, T), :] = columns

    def copies(field, number, orient):
        high, low = (0, NX5) if orient == 1 else (NX5, 0)
        last = rows + PAD
        pairs = [
            (field.at[pl.ds(high, NX5), :, pl.ds(rows, PAD), :], field.at[pl.ds(high, NX5), :, pl.ds(0, PAD), :], (right_x, me_y)),
            (field.at[pl.ds(low, NX5), :, pl.ds(PAD, PAD), :], field.at[pl.ds(low, NX5), :, pl.ds(last, PAD), :], (left_x, me_y)),
        ]
        for side, target in ((0, right_y), (1, left_y)):
            source, sink = edge.at[number, side], halo.at[number, side]
            pairs += [
                (source, sink.at[pl.ds(PAD, rows), :], (me_x, target)),
                (source.at[pl.ds(rows - PAD, PAD), :], sink.at[pl.ds(0, PAD), :], (right_x, target)),
                (source.at[pl.ds(0, PAD), :], sink.at[pl.ds(last, PAD), :], (left_x, target)),
            ]
        return [
            pltpu.make_async_remote_copy(
                src_ref=source,
                dst_ref=sink,
                send_sem=send_sem.at[number, n],
                recv_sem=recv_sem.at[number, n],
                device_id=target,
                device_id_type=MESH,
            )
            for n, (source, sink, target) in enumerate(pairs)
        ]

    def running(field, number, orient, i):
        pieces = []
        for q in range(Q):
            move_x, move_y, move_z = velocities[q]
            begin = i * T + PAD - orient * move_x
            if move_x == 0:
                begin = pl.multiple_of(begin, T)
            step = orient * move_y
            halves = []
            for z in range(2):
                from_z = (z + move_z) % 2
                tile = field[SLOT[q], from_z, pl.ds(begin, T), :]
                if step:
                    side = 0 if step == 1 else 1
                    k = 2 * SIDE_Y[move_y].index(q) + from_z
                    columns = halo[number, side, pl.ds(begin, T), :]
                    tile = pltpu.roll(tile, 1 if step == 1 else lanes - 1, 1)
                    tile = jnp.where(lane == (0 if step == 1 else lanes - 1), columns[:, k : k + 1], tile)
                halves.append(tile)
            pieces.append(jnp.concatenate(halves, axis=1))
        return pieces

    def own(i):
        begin = pl.multiple_of(i * T, T)
        return [both(lambda z: dist[q, z, pl.ds(begin, T), :]) for q in range(Q)]

    def solid_of(i):
        begin = pl.multiple_of(i * T, T)
        return both(lambda z: solid[z, pl.ds(begin, T), :]) > 0

    CH = 2 * H

    def dot(a, b):
        return jnp.dot(a, b, preferred_element_type=jnp.float32)

    def dot_t(a, b):
        return lax.dot_general(a, b, (((1,), (1,)), ((), ())), preferred_element_type=jnp.float32)

    def take(i, carry):
        begin = pl.multiple_of(i * T, T)
        put(cot_f, 0, -1, i, [both(lambda z: cot[q, z, pl.ds(begin, T), :]) for q in range(Q)])
        return carry

    lax.fori_loop(0, tiles, take, 0)
    pl.semaphore_wait(barrier, len(others))
    first = copies(cot_f, 0, -1)
    for copy in first:
        copy.start()

    def collide(i, carry):
        field = own(i)
        wide = widen(field, 1.0)
        for c in range(T * H // CH):
            part = slice(c * CH, (c + 1) * CH)
            saved[i, part, :] = jnp.tanh(dot(a_in[part, :], wide)).astype(jnp.bfloat16)
        out = dot(b_out[...], saved[i])
        is_solid = solid_of(i)
        posts = []
        for q in range(Q):
            at = slice(q * T, (q + 1) * T)
            value = field[q] + (out[at] + bias_out[at, :])
            value = jnp.where(is_solid, field[opposite[q]], value)
            posts.append(value.astype(jnp.bfloat16).astype(jnp.float32))
        put(post_f, 1, 1, i, posts)
        return carry

    lax.fori_loop(0, tiles, collide, 0, unroll=2)
    second = copies(post_f, 1, 1)
    for copy in second:
        copy.start()
    for copy in first + second:
        copy.wait()

    def backward(i, wide, grad, act_of):
        is_solid = solid_of(i)
        masked = [jnp.where(is_solid, 0.0, g) for g in grad]
        wide_out = widen(masked, 0.0)
        for c in range(T * H // CH):
            part = slice(c * CH, (c + 1) * CH)
            t = act_of(part)
            hid = dot(a_out[part, :], wide_out) * (1.0 - t * t)
            hid = hid.astype(jnp.bfloat16)
            hid_s[part, :] = hid
            acc_in[:, part] += dot_t(wide, hid)
        into = dot(b_in[...], hid_s[...])
        results = []
        for q in range(Q):
            at = slice(q * T, (q + 1) * T)
            acc_bias[at, :] += masked[q]
            results.append(masked[q] + into[at] + jnp.where(is_solid, grad[opposite[q]], 0.0))
        return wide_out, results

    def late(i, carry):
        wide = widen(running(post_f, 1, 1, i), 1.0)

        def act_of(part):
            t = jnp.tanh(dot(a_in[part, :], wide))
            act_s[part, :] = t.astype(jnp.bfloat16)
            return t

        wide_out, results = backward(i, wide, running(cot_f, 0, -1, i), act_of)
        for c in range(T * H // CH):
            part = slice(c * CH, (c + 1) * CH)
            acc_out[:, part] += dot_t(wide_out, act_s[part, :])
        put(mid_f, 2, -1, i, results)
        return carry

    lax.fori_loop(0, tiles, late, 0, unroll=2)
    third = copies(mid_f, 2, -1)
    for copy in third:
        copy.start()
    for copy in third:
        copy.wait()

    def early(i, carry):
        wide = widen(own(i), 1.0)
        wide_out, results = backward(
            i, wide, running(mid_f, 2, -1, i), lambda part: saved[i, part, :].astype(jnp.float32)
        )
        for c in range(T * H // CH):
            part = slice(c * CH, (c + 1) * CH)
            acc_out[:, part] += dot_t(wide_out, saved[i, part, :])
        begin = pl.multiple_of(i * T, T)
        for q in range(Q):
            for z in range(2):
                grad_start[q, z, pl.ds(begin, T), :] = results[q][:, z * lanes : (z + 1) * lanes]
        return carry

    lax.fori_loop(0, tiles, early, 0, unroll=2)

    tall = lax.broadcasted_iota(jnp.int32, (KA, H), 0) & (T - 1)

    def diagonal(acc):
        total = jnp.zeros((KA, H), jnp.float32)
        for s in range(T):
            total += jnp.where(tall == s, acc[:, s * H : (s + 1) * H], 0.0)
        return jnp.sum(total.reshape(KA // T, T, H), axis=1)

    part_x[...] = jnp.zeros_like(part_x)
    part_x[0 : KA // T, :] = diagonal(acc_out)
    part_x[24 : 24 + KA // T, :] = diagonal(acc_in)
    bias = jnp.sum(acc_bias[...], axis=1, keepdims=True)
    bias = jnp.broadcast_to(bias, (KQ, H)).reshape(Q, T, H)
    part_x[48 : 48 + Q, :] = jnp.sum(bias, axis=1)

    def gather(part, everyone, size, me, place, s_sem, r_sem):
        sends = [
            pltpu.make_async_remote_copy(
                src_ref=part,
                dst_ref=everyone.at[me],
                send_sem=s_sem.at[d - 1],
                recv_sem=r_sem.at[d - 1],
                device_id=place(lax.rem(me + d, size)),
                device_id_type=MESH,
            )
            for d in range(1, size)
        ]
        for copy in sends:
            copy.start()
        everyone[me] = part[...]
        for copy in sends:
            copy.wait()
        total = everyone[0]
        for d in range(1, size):
            total = total + everyone[d]
        return total

    part_y[...] = gather(part_x, all_x, nx, me_x, lambda a: (a, me_y), sx_sem, rx_sem)
    sums = gather(part_y, all_y, ny, me_y, lambda b: (me_x, b), sy_sem, ry_sem) * factor
    grad_weight_in[...] = sums[24 : 24 + Q]
    grad_bias_in[...] = sums[24 + Q : 25 + Q]

    def across(part):
        return jnp.transpose(jnp.concatenate([part, jnp.zeros((H - 24, H), jnp.float32)], axis=0))

    grad_weight_out[...] = across(sums[0:24])[:, :Q]
    grad_bias_out[...] = across(sums[48:72])[0:1, :Q]


def shards(dist_start, cotangent, solid_mask, weight_in, bias_in, weight_out, bias_out):
    nx, ny = lax.axis_size("gx"), lax.axis_size("gy")
    H = weight_in.shape[1]
    rows, lanes = dist_start.shape[2:]
    tiles = rows // T
    f32, bf16 = jnp.float32, jnp.bfloat16
    factor = 1.0 / math.sqrt(solid_mask.size * nx * ny)

    field = pltpu.VMEM((Q, 2, rows + 2 * PAD, lanes), f32)
    vmem = pl.BlockSpec(memory_space=pltpu.VMEM)
    dma = pltpu.SemaphoreType.DMA
    grad_start, d_weight_in, d_bias_in, d_weight_out, d_bias_out = pl.pallas_call(
        functools.partial(kernel, nx, ny, factor),
        out_shape=(
            jax.ShapeDtypeStruct(dist_start.shape, f32),
            jax.ShapeDtypeStruct((Q, H), f32),
            jax.ShapeDtypeStruct((1, H), f32),
            jax.ShapeDtypeStruct((H, Q), f32),
            jax.ShapeDtypeStruct((1, Q), f32),
        ),
        in_specs=[vmem] * 7,
        out_specs=(vmem,) * 5,
        scratch_shapes=[
            field,
            field,
            field,
            pltpu.VMEM((3, 2, rows, lanes), f32),
            pltpu.VMEM((3, 2, rows + 2 * PAD, lanes), f32),
            pltpu.VMEM((tiles, T * H, 2 * lanes), bf16),
            pltpu.VMEM((T * H, KA), bf16),
            pltpu.VMEM((T * H, KA), bf16),
            pltpu.VMEM((KQ, T * H), bf16),
            pltpu.VMEM((KQ, T * H), bf16),
            pltpu.VMEM((T * H, 2 * lanes), bf16),
            pltpu.VMEM((T * H, 2 * lanes), bf16),
            pltpu.VMEM((KA, T * H), f32),
            pltpu.VMEM((KA, T * H), f32),
            pltpu.VMEM((KQ, 2 * lanes), f32),
            pltpu.VMEM((KQ, 2 * lanes), f32),
            pltpu.VMEM((72, H), f32),
            pltpu.VMEM((72, H), f32),
            pltpu.VMEM((nx, 72, H), f32),
            pltpu.VMEM((ny, 72, H), f32),
            dma((3, 8)),
            dma((3, 8)),
            dma((nx - 1,)),
            dma((nx - 1,)),
            dma((ny - 1,)),
            dma((ny - 1,)),
        ],
        compiler_params=pltpu.CompilerParams(
            collective_id=0, has_side_effects=True, vmem_limit_bytes=60 * 1024 * 1024
        ),
    )(dist_start, cotangent, solid_mask, weight_in, bias_in[None], weight_out, bias_out[None])
    return grad_start, d_weight_in, d_bias_in[0], d_weight_out, d_bias_out[0]


def solution(mesh):
    placed = (
        P(None, None, "gx", "gy"),
        P(None, None, "gx", "gy"),
        P(None, "gx", "gy"),
        P(),
        P(),
        P(),
        P(),
    )
    return jax.shard_map(
        shards,
        mesh=mesh,
        in_specs=placed,
        out_specs=(P(None, None, "gx", "gy"), P(), P(), P(), P()),
        check_vma=False,
    )
```
